512 devices in a mesh: rep: 64 (over x_lo, z, core), fsdp: 8 (over y, x_hi).
Axes of the slice: x: 4 (x_hi: 2, x_lo: 2; x = x_hi * 2 + x_lo), y: 4, z: 16, core: 2. Of those that a mesh axis runs over, the one named last changes fastest.
Arguments:
- hidden_in: bfloat16 [64, 1536, 4096], P('rep', 'fsdp'), may hold values from -6 to 6
- cotangent: bfloat16 [64, 1536, 512], P('rep', 'fsdp'), may hold values from -6 to 6
- weights: float32 [64, 4096, 512], P('rep', 'fsdp'), may hold values from -6 to 6
- moments: bfloat16 [64, 4096, 512], P('rep', 'fsdp'), may hold values from -6 to 6
- norm_gains: bfloat16 [64, 4096], P('rep', 'fsdp'), may hold values from 0.099609375 to 1.8984375
- gain_moments: bfloat16 [64, 4096], P('rep', 'fsdp'), may hold values from -60 to 60
- step_count: int32 [], replicated, may hold values from 0 to 99999
Outputs:
- new_weights: float32 [64, 4096, 512], P('rep', 'fsdp')
- new_moments: bfloat16 [64, 4096, 512], P('rep', 'fsdp')
- new_gains: bfloat16 [64, 4096], P('rep', 'fsdp')
- new_gain_moments: bfloat16 [64, 4096], P('rep', 'fsdp')
The draws below stay inside these ranges and needn't reach their ends.
All inputs are finite; a program needn't handle non-finite values.
Results may differ from the reference program's by a relative error of at most 0.0061.
Values may be sent and summed in bfloat16 or wider, within the bound.
No kernel may reach another device: no remote copies, remote signals or barrier semaphores. Data moves between devices by JAX's collectives and lax.ppermute only.
A program may use at most 128 MiB of HBM per device.

```python
import jax
import jax.numpy as jnp
from jax import lax

D = 4096
KV = 512
TOKR = 1536
REPS = 64


def strengthened(drawn, key, source, target, blocks, factor):
    owner, partner = [(jnp.arange(drawn.shape[position]) // (drawn.shape[position] // blocks)).reshape([-1 if axis == position else 1 for axis in range(drawn.ndim)]) for position in (source, target)]
    chosen = jax.random.permutation(key, blocks)[partner]
    strong = (owner == chosen) | (owner == (partner + blocks // 2) % blocks)
    return jnp.where(strong, factor * drawn, drawn)


def shard_levels(rng, shape, shards, least, high):
    factor_of, own = 1.0, jax.random.fold_in(rng, 6)
    for axis_at, parts in shards:
        heights = jnp.exp(jax.random.uniform(jax.random.fold_in(own, axis_at), (parts,), jnp.float32, least / len(shards), high / len(shards)))
        factor_of = factor_of * jnp.repeat(heights, shape[axis_at] // parts).reshape([-1 if axis == axis_at else 1 for axis in range(len(shape))])
    return factor_of


def centred(key, extent, deviation, bound, cuts=(), kind=jnp.bfloat16):
    array = jax.random.normal(key, extent, jnp.float32) * deviation
    if len(cuts) > 0:
        array = shard_levels(key, extent, cuts, -0.22, 0.18) * array
    return jnp.clip(array, min=-bound, max=bound).astype(kind)


def gaussian_with(rng, dims, deviation, limit, cuts, heavy, held_as=jnp.bfloat16):
    array = deviation * jax.random.normal(rng, dims, jnp.float32)
    if cuts:
        array = array * shard_levels(rng, dims, cuts, -0.22, 0.18)
    return jnp.clip(strengthened(array, jax.random.fold_in(rng, 3), *heavy), -limit, limit).astype(held_as)


def setup_inputs(seed: int = 0) -> dict:
    key_of = jax.random.split(jax.random.key(seed), 8)
    hidden_in = gaussian_with(key_of[0], (REPS, TOKR, D), 1.0, 6.0, ((0, 64), (1, 8)), (1, 2, 8, 2.0))
    cotangent = centred(key_of[1], (REPS, TOKR, KV), 1.0, 6.0, ((0, 64), (1, 8)))
    weights = centred(key_of[2], (REPS, D, KV), 1.0, 6.0, ((0, 64), (1, 8)), jnp.float32)
    moments = centred(key_of[3], (REPS, D, KV), 1.0, 6.0, ((0, 64), (1, 8)))
    norm_gains = jnp.clip(1.0 + 0.18 * jax.random.normal(key_of[4], (REPS, D), jnp.float32), 0.099609375, 1.8984375).astype(jnp.bfloat16)
    gain_moments = centred(key_of[5], (REPS, D), 10.0, 60.0, ((0, 64), (1, 8)))
    step_count = jax.random.randint(key_of[6], (), 0, 100000).astype(jnp.int32)
    return dict(hidden_in=hidden_in, cotangent=cotangent, weights=weights, moments=moments, norm_gains=norm_gains, gain_moments=gain_moments, step_count=step_count)


norm_eps = 1e-05
momentum_beta = 0.9
learn_weight = 0.25
learn_gain = 0.01

def replica_update(bundle):
    tokens_blk, upstream, master, moment, norm_gain, gain_moment = bundle
    tokens_f = tokens_blk.astype(jnp.float32)
    inv_rms = lax.rsqrt(lax.optimization_barrier(jnp.mean(tokens_f * tokens_f, axis=-1, keepdims=True)) + norm_eps)
    normed = (tokens_f * inv_rms).astype(jnp.bfloat16)
    scaled_in = (normed.astype(jnp.float32) * norm_gain.astype(jnp.float32)).astype(jnp.bfloat16)
    grad_scale = D ** (-0.5)
    grad_w = grad_scale * lax.dot_general(scaled_in, upstream, (((0,), (0,)), ((), ())), preferred_element_type=jnp.float32)
    weights_bf = master.astype(jnp.bfloat16)
    grad_in = grad_scale * lax.dot_general(upstream, weights_bf, (((1,), (1,)), ((), ())), preferred_element_type=jnp.float32)
    grad_gain = lax.optimization_barrier(jnp.sum(normed.astype(jnp.float32) * grad_in, axis=0))
    mom_w = (momentum_beta * moment.astype(jnp.float32) + grad_w).astype(jnp.bfloat16)
    mom_g = (momentum_beta * gain_moment.astype(jnp.float32) + grad_gain).astype(jnp.bfloat16)
    stepped_w = master - learn_weight * mom_w.astype(jnp.float32)
    stepped_g = (norm_gain.astype(jnp.float32) - learn_gain * mom_g.astype(jnp.float32)).astype(jnp.bfloat16)
    return (stepped_w, mom_w, stepped_g, mom_g)

def average_pair(values, partner):
    other = jnp.take(values, partner, axis=0)
    return 0.5 * (values.astype(jnp.float32) + other.astype(jnp.float32))

def reference(hidden_in, cotangent, weights, moments, norm_gains, gain_moments, step_count):
    stepped_w, mom_w, stepped_g, mom_g = lax.map(replica_update, (hidden_in, cotangent, weights, moments, norm_gains, gain_moments))
    hop_total = REPS.bit_length() - 1
    hop_size = jnp.left_shift(jnp.int32(1), jnp.mod(step_count.astype(jnp.int32), hop_total).astype(jnp.int32)).astype(jnp.int32)
    partner = jnp.mod(jnp.arange(REPS, dtype=jnp.int32) + hop_size, REPS).astype(jnp.int32)
    new_weights = average_pair(stepped_w, partner)
    new_moments = average_pair(mom_w, partner).astype(jnp.bfloat16)
    new_gains = average_pair(stepped_g, partner).astype(jnp.bfloat16)
    new_gain_moments = average_pair(mom_g, partner).astype(jnp.bfloat16)
    return (new_weights, new_moments, new_gains, new_gain_moments)
```

```python
from functools import partial

import jax
import jax.numpy as jnp
from jax import lax
from jax.experimental import pallas as pl
from jax.experimental.pallas import tpu as pltpu
from jax.sharding import PartitionSpec as P

D = 4096

norm_eps = 1e-05
momentum_beta = 0.9
learn_weight = 0.25
learn_gain = 0.01
grad_scale = D ** (-0.5)

EXTRA = 16
ROWS = 32
f32, bf16 = jnp.float32, jnp.bfloat16


def shifted(value, axis, steps):
    count = lax.axis_size(axis)
    pairs = [(source, (source + steps) % count) for source in range(count)]
    return lax.ppermute(value, axis, pairs)


def early_kernel(master_ref, gain_ref, out_ref):
    rows = master_ref.shape[0]
    out_ref[:rows, :] = master_ref[...].astype(bf16)
    out_ref[rows:, :] = jnp.broadcast_to(gain_ref[...], (EXTRA, out_ref.shape[1]))


def pack_kernel(hidden_ref, cotangent_ref, out_ref):
    parts, _, width = out_ref.shape
    share = hidden_ref.shape[1] // parts
    hidden = hidden_ref[...].astype(f32)
    inv_rms = lax.rsqrt(jnp.mean(hidden * hidden, axis=-1, keepdims=True) + norm_eps)
    cotangent = cotangent_ref[...]
    for part in range(parts):
        block = hidden_ref[:, part * share : (part + 1) * share].astype(f32)
        out_ref[part, :, :share] = (block * inv_rms).astype(bf16)
        out_ref[part, :, share:] = cotangent


def grad_kernel(got_ref, master_ref, moment_ref, gain_ref, gain_moment_ref, out_ref, acc_ref):
    step = pl.program_id(0)
    rows = master_ref.shape[0]

    @pl.when(step == 0)
    def _():
        acc_ref[...] = jnp.zeros_like(acc_ref)

    acc_ref[...] += lax.dot_general(
        got_ref[:, :rows],
        got_ref[:, rows:],
        (((0,), (0,)), ((), ())),
        preferred_element_type=f32,
    )

    @pl.when(step == pl.num_programs(0) - 1)
    def _():
        total = grad_scale * acc_ref[...]
        gain = jnp.transpose(jnp.broadcast_to(gain_ref[...].astype(f32), (128, rows)))[:, :1]
        mom = momentum_beta * moment_ref[...].astype(f32) + gain * total
        out_ref[:rows, :] = mom.astype(bf16)
        add_gain = jnp.sum(master_ref[...].astype(bf16).astype(f32) * total, axis=1, keepdims=True)
        add_gain = jnp.transpose(jnp.broadcast_to(add_gain, (rows, 128)))[:1, :]
        mom_g = momentum_beta * gain_moment_ref[...].astype(f32) + add_gain
        out_ref[rows:, :] = jnp.broadcast_to(mom_g, (EXTRA, rows)).astype(bf16)


def final_kernel(
    master_ref, gain_ref, mom_ref, peer_early_ref, peer_mom_ref,
    out_w_ref, out_mom_ref, out_gain_ref, out_gain_mom_ref,
):
    step = pl.program_id(0)
    rows, block = master_ref.shape[0], out_w_ref.shape[0]
    here = pl.ds(pl.multiple_of(step * block, block), block)
    mom = mom_ref[here, :].astype(f32)
    peer_mom = peer_mom_ref[here, :].astype(f32)
    stepped = master_ref[here, :] - learn_weight * mom
    peer_stepped = peer_early_ref[here, :].astype(f32) - learn_weight * peer_mom
    out_w_ref[...] = 0.5 * (stepped + peer_stepped)
    out_mom_ref[...] = (0.5 * (mom + peer_mom)).astype(bf16)

    @pl.when(step == 0)
    def _():
        mom_g = mom_ref[rows : rows + EXTRA, :].astype(f32)[:1, :]
        peer_mom_g = peer_mom_ref[rows : rows + EXTRA, :].astype(f32)[:1, :]
        peer_gain = peer_early_ref[rows : rows + EXTRA, :].astype(f32)[:1, :]
        own = (gain_ref[...].astype(f32) - learn_gain * mom_g).astype(bf16).astype(f32)
        peer = (peer_gain - learn_gain * peer_mom_g).astype(bf16).astype(f32)
        out_gain_ref[...] = (0.5 * (own + peer)).astype(bf16)
        out_gain_mom_ref[...] = (0.5 * (mom_g + peer_mom_g)).astype(bf16)


def whole(distance, hidden_in, cotangent, weights, moments, norm_gains, gain_moments):
    inputs, upstream, master, moment = hidden_in[0], cotangent[0], weights[0], moments[0]
    tokens, width = inputs.shape
    rows, kv = master.shape
    parts = lax.axis_size("fsdp")
    early = pl.pallas_call(
        early_kernel,
        out_shape=jax.ShapeDtypeStruct((rows + EXTRA, kv), bf16),
        name="early",
    )(master, norm_gains)
    peer_early = shifted(early, "rep", -distance)

    packed = pl.pallas_call(
        pack_kernel,
        grid=(tokens // ROWS,),
        in_specs=[
            pl.BlockSpec((ROWS, width), lambda i: (i, 0)),
            pl.BlockSpec((ROWS, kv), lambda i: (i, 0)),
        ],
        out_specs=pl.BlockSpec((parts, ROWS, rows + kv), lambda i: (0, i, 0)),
        out_shape=jax.ShapeDtypeStruct((parts, tokens, rows + kv), bf16),
        name="pack",
    )(inputs, upstream)
    got = lax.all_to_all(packed, "fsdp", split_axis=0, concat_axis=0, tiled=True)
    got = got.reshape(parts * tokens, rows + kv)

    depth = 256
    fixed = lambda shape: pl.BlockSpec(shape, lambda i: (0, 0))
    mom = pl.pallas_call(
        grad_kernel,
        grid=(parts * tokens // depth,),
        in_specs=[
            pl.BlockSpec((depth, rows + kv), lambda i: (i, 0)),
            fixed((rows, kv)),
            fixed((rows, kv)),
            fixed((1, rows)),
            fixed((1, rows)),
        ],
        out_specs=fixed((rows + EXTRA, kv)),
        out_shape=jax.ShapeDtypeStruct((rows + EXTRA, kv), bf16),
        scratch_shapes=[pltpu.VMEM((rows, kv), f32)],
        name="grad",
    )(got, master, moment, norm_gains, gain_moments)
    peer_mom = shifted(mom, "rep", -distance)

    return mom, peer_early, peer_mom


def shards(hidden_in, cotangent, weights, moments, norm_gains, gain_moments, step_count):
    hop_total = lax.axis_size("rep").bit_length() - 1
    hop_index = lax.rem(step_count, hop_total)
    branches = [partial(whole, 1 << level) for level in range(hop_total)]
    mom, peer_early, peer_mom = lax.switch(
        hop_index, branches, hidden_in, cotangent, weights, moments, norm_gains, gain_moments
    )
    master = weights[0]
    rows, kv = master.shape
    block = rows // 4
    tile = pl.BlockSpec((block, kv), lambda i: (i, 0))
    row = pl.BlockSpec((1, rows), lambda i: (0, 0))
    out_w, out_mom, out_gain, out_gain_mom = pl.pallas_call(
        final_kernel,
        grid=(rows // block,),
        in_specs=[pl.BlockSpec(memory_space=pltpu.VMEM)] * 5,
        out_specs=[tile, tile, row, row],
        out_shape=[
            jax.ShapeDtypeStruct((rows, kv), f32),
            jax.ShapeDtypeStruct((rows, kv), bf16),
            jax.ShapeDtypeStruct((1, rows), bf16),
            jax.ShapeDtypeStruct((1, rows), bf16),
        ],
        name="final",
    )(master, norm_gains, mom, peer_early, peer_mom)
    return (out_w[None], out_mom[None], out_gain, out_gain_mom)


def solution(mesh):
    in_specs = (
        P("rep", "fsdp", None),
        P("rep", "fsdp", None),
        P("rep", "fsdp", None),
        P("rep", "fsdp", None),
        P("rep", "fsdp"),
        P("rep", "fsdp"),
        P(),
    )
    out_specs = (P("rep", "fsdp", None), P("rep", "fsdp", None), P("rep", "fsdp"), P("rep", "fsdp"))
    return jax.shard_map(shards, mesh=mesh, in_specs=in_specs, out_specs=out_specs, check_vma=False)
```

```python
from functools import partial

import jax
import jax.numpy as jnp
from jax import lax
from jax.experimental import pallas as pl
from jax.experimental.pallas import tpu as pltpu
from jax.sharding import PartitionSpec as P

D = 4096

norm_eps = 1e-05
momentum_beta = 0.9
learn_weight = 0.25
learn_gain = 0.01
grad_scale = D ** (-0.5)

EXTRA = 16
ROWS = 96
f32, bf16 = jnp.float32, jnp.bfloat16


def from_peer(value, steps):
    count = lax.axis_size("rep")
    return lax.ppermute(value, "rep", [(source, (source - steps) % count) for source in range(count)])


def within_halves(value, steps):
    half = lax.axis_size("rep") // 2
    pairs = [(h * half + i, h * half + (i - steps) % half) for h in range(2) for i in range(half)]
    return lax.ppermute(value, "rep", pairs)


def swap_halves(value, steps):
    half = lax.axis_size("rep") // 2
    pairs = [
        (h * half + i, (1 - h if i + steps >= half else h) * half + i)
        for h in range(2)
        for i in range(half)
    ]
    return lax.ppermute(value, "rep", pairs)


def early_kernel(master_ref, gain_ref, out_ref):
    rows = master_ref.shape[0]
    out_ref[:rows, :] = master_ref[...].astype(bf16)
    out_ref[rows:, :] = jnp.broadcast_to(gain_ref[...], (EXTRA, out_ref.shape[1]))


def pack_kernel(hidden_ref, cotangent_ref, out_ref):
    parts = out_ref.shape[0]
    share = hidden_ref.shape[1] // parts
    hidden = hidden_ref[...].astype(f32)
    inv_rms = lax.rsqrt(jnp.mean(hidden * hidden, axis=-1, keepdims=True) + norm_eps)
    cotangent = cotangent_ref[...]
    for part in range(parts):
        block = hidden_ref[:, part * share : (part + 1) * share].astype(f32)
        out_ref[part, :, :share] = (block * inv_rms).astype(bf16)
        out_ref[part, :, share:] = cotangent


def grad_kernel(got_ref, master_ref, moment_ref, gain_ref, gain_moment_ref, out_ref):
    rows = master_ref.shape[0]
    total = grad_scale * lax.dot_general(
        got_ref[:, :rows],
        got_ref[:, rows:],
        (((0,), (0,)), ((), ())),
        preferred_element_type=f32,
    )
    gain = jnp.transpose(jnp.broadcast_to(gain_ref[...].astype(f32), (128, rows)))[:, :1]
    mom = momentum_beta * moment_ref[...].astype(f32) + gain * total
    out_ref[:rows, :] = mom.astype(bf16)
    add_gain = jnp.sum(master_ref[...].astype(bf16).astype(f32) * total, axis=1, keepdims=True)
    add_gain = jnp.transpose(jnp.broadcast_to(add_gain, (rows, 128)))[:1, :]
    mom_g = momentum_beta * gain_moment_ref[...].astype(f32) + add_gain
    out_ref[rows:, :] = jnp.broadcast_to(mom_g, (EXTRA, rows)).astype(bf16)


def own_step_kernel(master_ref, mom_ref, out_ref):
    rows = master_ref.shape[0]
    out_ref[...] = 0.5 * (master_ref[...] - learn_weight * mom_ref[:rows, :].astype(f32))


def final_kernel(
    own_ref, mom_ref, peer_early_ref, peer_mom_ref, gain_ref, peer_gain_ref, mom_g_ref, peer_mom_g_ref,
    out_w_ref, out_mom_ref, out_gain_ref, out_gain_mom_ref,
):
    peer_mom = peer_mom_ref[...].astype(f32)
    peer_step = peer_early_ref[...].astype(f32) - learn_weight * peer_mom
    out_w_ref[...] = own_ref[...] + 0.5 * peer_step
    out_mom_ref[...] = (0.5 * (mom_ref[...].astype(f32) + peer_mom)).astype(bf16)

    @pl.when(pl.program_id(0) == 0)
    def _():
        mom_g = mom_g_ref[...].astype(f32)[:1, :]
        peer_mom_g = peer_mom_g_ref[...].astype(f32)[:1, :]
        peer_gain = peer_gain_ref[...].astype(f32)[:1, :]
        own = (gain_ref[...].astype(f32) - learn_gain * mom_g).astype(bf16).astype(f32)
        peer = (peer_gain - learn_gain * peer_mom_g).astype(bf16).astype(f32)
        out_gain_ref[...] = (0.5 * (own + peer)).astype(bf16)
        out_gain_mom_ref[...] = (0.5 * (mom_g + peer_mom_g)).astype(bf16)


VMEM = pl.BlockSpec(memory_space=pltpu.VMEM)


def whole(distance, hidden_in, cotangent, weights, moments, norm_gains, gain_moments):
    inputs, upstream, master, moment = hidden_in[0], cotangent[0], weights[0], moments[0]
    tokens, width = inputs.shape
    rows, kv = master.shape
    parts = lax.axis_size("fsdp")
    far = distance * 2 == lax.axis_size("rep")
    far_along = 8 <= distance and not far
    early = pl.pallas_call(
        early_kernel,
        out_shape=jax.ShapeDtypeStruct((rows + EXTRA, kv), bf16),
        name="early",
    )(master, norm_gains)
    peer_early = from_peer(early, distance) if far else within_halves(early, distance)

    packed = pl.pallas_call(
        pack_kernel,
        grid=(tokens // ROWS,),
        in_specs=[
            pl.BlockSpec((ROWS, width), lambda i: (i, 0)),
            pl.BlockSpec((ROWS, kv), lambda i: (i, 0)),
        ],
        out_specs=pl.BlockSpec((parts, ROWS, rows + kv), lambda i: (0, i, 0)),
        out_shape=jax.ShapeDtypeStruct((parts, tokens, rows + kv), bf16),
        name="pack",
    )(inputs, upstream)
    got = lax.all_to_all(packed, "fsdp", split_axis=0, concat_axis=0, tiled=True)
    if not far and not far_along:
        peer_early, got = lax.optimization_barrier((peer_early, got))
        peer_early = swap_halves(peer_early, distance)
    got = pltpu.with_memory_space_constraint(got.reshape(parts * tokens, rows + kv), pltpu.VMEM)

    mom = pl.pallas_call(
        grad_kernel,
        in_specs=[VMEM] * 5,
        out_specs=VMEM,
        out_shape=jax.ShapeDtypeStruct((rows + EXTRA, kv), bf16),
        name="grad",
    )(got, master, moment, norm_gains, gain_moments)
    if far_along:
        peer_early, mom = lax.optimization_barrier((peer_early, mom))
        peer_early = swap_halves(peer_early, distance)
    peer_mom = from_peer(mom, distance)
    own = pl.pallas_call(
        own_step_kernel,
        out_shape=jax.ShapeDtypeStruct((rows, kv), f32),
        name="own",
    )(master, mom)
    return own, mom, peer_mom, peer_early


def shards(hidden_in, cotangent, weights, moments, norm_gains, gain_moments, step_count):
    hop_total = lax.axis_size("rep").bit_length() - 1
    hop_index = lax.rem(step_count, hop_total)
    branches = [partial(whole, 1 << level) for level in range(hop_total)]
    own, mom, peer_mom, peer_early = lax.switch(
        hop_index, branches, hidden_in, cotangent, weights, moments, norm_gains, gain_moments
    )
    rows, kv = own.shape
    block = rows // 2
    tile = pl.BlockSpec((block, kv), lambda i: (i, 0))
    row = pl.BlockSpec((1, rows), lambda i: (0, 0))
    last = pl.BlockSpec((EXTRA, kv), lambda i: (rows // EXTRA, 0))
    out_w, out_mom, out_gain, out_gain_mom = pl.pallas_call(
        final_kernel,
        grid=(rows // block,),
        in_specs=[tile, tile, tile, tile, row, last, last, last],
        out_specs=[tile, tile, row, row],
        out_shape=[
            jax.ShapeDtypeStruct((rows, kv), f32),
            jax.ShapeDtypeStruct((rows, kv), bf16),
            jax.ShapeDtypeStruct((1, rows), bf16),
            jax.ShapeDtypeStruct((1, rows), bf16),
        ],
        name="final",
    )(own, mom, peer_early, peer_mom, norm_gains, peer_early, mom, peer_mom)
    return (out_w[None], out_mom[None], out_gain, out_gain_mom)


def solution(mesh):
    in_specs = (
        P("rep", "fsdp", None),
        P("rep", "fsdp", None),
        P("rep", "fsdp", None),
        P("rep", "fsdp", None),
        P("rep", "fsdp"),
        P("rep", "fsdp"),
        P(),
    )
    out_specs = (P("rep", "fsdp", None), P("rep", "fsdp", None), P("rep", "fsdp"), P("rep", "fsdp"))
    return jax.shard_map(shards, mesh=mesh, in_specs=in_specs, out_specs=out_specs, check_vma=False)
```

```python
from functools import partial

import jax
import jax.numpy as jnp
from jax import lax
from jax.experimental import pallas as pl
from jax.experimental.pallas import tpu as pltpu
from jax.sharding import PartitionSpec as P

D = 4096

norm_eps = 1e-05
momentum_beta = 0.9
learn_weight = 0.25
learn_gain = 0.01
grad_scale = D ** (-0.5)

EXTRA = 8
ROWS = 96
f32, bf16 = jnp.float32, jnp.bfloat16


def from_peer(value, steps):
    count = lax.axis_size("rep")
    return lax.ppermute(value, "rep", [(source, (source - steps) % count) for source in range(count)])


def within_halves(value, steps):
    half = lax.axis_size("rep") // 2
    pairs = [(h * half + i, h * half + (i - steps) % half) for h in range(2) for i in range(half)]
    return lax.ppermute(value, "rep", pairs)


def swap_halves(value, low, high):
    half = lax.axis_size("rep") // 2
    pairs = [(h * half + i, (1 - h) * half + i) for h in range(2) for i in range(low, high)]
    place = lax.rem(lax.axis_index("rep"), half)
    took = (place >= low) & (place < high)
    return lax.ppermute(value, "rep", pairs), took.astype(jnp.int32).reshape(1)


def early_kernel(master_ref, gain_ref, out_ref):
    rows = master_ref.shape[0]
    out_ref[:rows, :] = master_ref[...].astype(bf16)
    out_ref[rows:, :] = jnp.broadcast_to(gain_ref[...], (EXTRA, out_ref.shape[1]))


def pack_kernel(hidden_ref, cotangent_ref, out_ref):
    parts = out_ref.shape[0]
    share = hidden_ref.shape[1] // parts
    hidden = hidden_ref[...].astype(f32)
    inv_rms = lax.rsqrt(jnp.mean(hidden * hidden, axis=-1, keepdims=True) + norm_eps)
    cotangent = cotangent_ref[...]
    for part in range(parts):
        block = hidden_ref[:, part * share : (part + 1) * share].astype(f32)
        out_ref[part, :, :share] = (block * inv_rms).astype(bf16)
        out_ref[part, :, share:] = cotangent


def grad_kernel(got_ref, master_ref, moment_ref, gain_ref, gain_moment_ref, out_ref):
    rows = master_ref.shape[0]
    total = grad_scale * lax.dot_general(
        got_ref[:, :rows],
        got_ref[:, rows:],
        (((0,), (0,)), ((), ())),
        preferred_element_type=f32,
    )
    gain = jnp.transpose(jnp.broadcast_to(gain_ref[...].astype(f32), (128, rows)))[:, :1]
    mom = momentum_beta * moment_ref[...].astype(f32) + gain * total
    out_ref[:rows, :] = mom.astype(bf16)
    add_gain = jnp.sum(master_ref[...].astype(bf16).astype(f32) * total, axis=1, keepdims=True)
    add_gain = jnp.transpose(jnp.broadcast_to(add_gain, (rows, 128)))[:1, :]
    mom_g = momentum_beta * gain_moment_ref[...].astype(f32) + add_gain
    out_ref[rows:, :] = jnp.broadcast_to(mom_g, (EXTRA, rows)).astype(bf16)


def own_step_kernel(master_ref, mom_ref, out_ref):
    rows = master_ref.shape[0]
    out_ref[...] = 0.5 * (master_ref[...] - learn_weight * mom_ref[:rows, :].astype(f32))


def final_kernel(
    took_ref, own_ref, mom_ref, kept_ref, swapped_ref, peer_mom_ref,
    gain_ref, kept_gain_ref, swapped_gain_ref, mom_g_ref, peer_mom_g_ref,
    out_w_ref, out_mom_ref, out_gain_ref, out_gain_mom_ref,
):
    peer_mom = peer_mom_ref[...].astype(f32)
    out_mom_ref[...] = (0.5 * (mom_ref[...].astype(f32) + peer_mom)).astype(bf16)

    def finish(early_ref, early_gain_ref):
        peer_step = early_ref[...].astype(f32) - learn_weight * peer_mom
        out_w_ref[...] = own_ref[...] + 0.5 * peer_step

        @pl.when(pl.program_id(0) == 0)
        def _():
            mom_g = mom_g_ref[...].astype(f32)[:1, :]
            peer_mom_g = peer_mom_g_ref[...].astype(f32)[:1, :]
            peer_gain = early_gain_ref[...].astype(f32)[:1, :]
            own = (gain_ref[...].astype(f32) - learn_gain * mom_g).astype(bf16).astype(f32)
            peer = (peer_gain - learn_gain * peer_mom_g).astype(bf16).astype(f32)
            out_gain_ref[...] = (0.5 * (own + peer)).astype(bf16)
            out_gain_mom_ref[...] = (0.5 * (mom_g + peer_mom_g)).astype(bf16)

    pl.when(took_ref[0] == 0)(partial(finish, kept_ref, kept_gain_ref))
    pl.when(took_ref[0] != 0)(partial(finish, swapped_ref, swapped_gain_ref))


VMEM = pl.BlockSpec(memory_space=pltpu.VMEM)


def whole(distance, hidden_in, cotangent, weights, moments, norm_gains, gain_moments, step_count):
    inputs, upstream, master, moment = hidden_in[0], cotangent[0], weights[0], moments[0]
    tokens, width = inputs.shape
    rows, kv = master.shape
    parts = lax.axis_size("fsdp")
    far = distance * 2 == lax.axis_size("rep")
    far_along = 8 <= distance and not far
    early = pl.pallas_call(
        early_kernel,
        out_shape=jax.ShapeDtypeStruct((rows + EXTRA, kv), bf16),
        name="early",
    )(master, norm_gains)
    half = lax.axis_size("rep") // 2
    peer_early = from_peer(early, distance) if far else within_halves(early, distance)

    def own_step(master, mom):
        return pl.pallas_call(
            own_step_kernel,
            out_shape=jax.ShapeDtypeStruct((rows, kv), f32),
            name="own",
        )(master, mom)

    def between(first, master, mom, peer_early):
        if first:
            peer_early, master = lax.optimization_barrier((peer_early, master))
        swapped, took = swap_halves(peer_early, half - distance, half)
        return own_step(master, mom), swapped, took

    def section(block, *operands):
        inputs, upstream, master, moment, norm_gains, gain_moments = operands[:6]
        packed = pl.pallas_call(
            pack_kernel,
            grid=(tokens // block,),
            in_specs=[
                pl.BlockSpec((block, width), lambda i: (i, 0)),
                pl.BlockSpec((block, kv), lambda i: (i, 0)),
            ],
            out_specs=pl.BlockSpec((parts, block, rows + kv), lambda i: (0, i, 0)),
            out_shape=jax.ShapeDtypeStruct((parts, tokens, rows + kv), bf16),
            name="pack",
        )(inputs, upstream)
        got = lax.all_to_all(packed, "fsdp", split_axis=0, concat_axis=0, tiled=True)
        got = got.reshape(parts * tokens, rows + kv)
        early = operands[6:]
        if early:
            got, *early = lax.optimization_barrier((got, *early))
        got = pltpu.with_memory_space_constraint(got, pltpu.VMEM)
        mom = pl.pallas_call(
            grad_kernel,
            in_specs=[VMEM] * 5,
            out_specs=VMEM,
            out_shape=jax.ShapeDtypeStruct((rows + EXTRA, kv), bf16),
            name="grad",
        )(got, master, moment, norm_gains, gain_moments)
        return (mom, *early)

    operands = (inputs, upstream, master, moment, norm_gains, gain_moments)
    if far_along:
        (mom,) = section(ROWS, *operands)
        peer_mom = from_peer(mom, distance)
        sure = step_count >= 0
        own, swapped, took = lax.cond(
            sure, partial(between, True), partial(between, False), master, mom, peer_early
        )
        peer_mom, own = lax.optimization_barrier((peer_mom, own))
    elif far:
        (mom,) = section(ROWS, *operands)
        swapped, took = early, jnp.zeros((1,), jnp.int32)
    else:
        mom, peer_early = section(ROWS, *operands, peer_early)
        swapped, took = swap_halves(peer_early, half - distance, half)
        if distance == 2:
            peer_early, took = jnp.where(took != 0, swapped, peer_early), jnp.zeros_like(took)
    if not far_along:
        peer_mom = from_peer(mom, distance)
        own = own_step(master, mom)
    return own, mom, peer_mom, peer_early, swapped, took


def shards(hidden_in, cotangent, weights, moments, norm_gains, gain_moments, step_count):
    hop_total = lax.axis_size("rep").bit_length() - 1
    hop_index = lax.rem(step_count, hop_total)
    branches = [partial(whole, 1 << level) for level in range(hop_total)]
    own, mom, peer_mom, peer_early, swapped, took = lax.switch(
        hop_index, branches, hidden_in, cotangent, weights, moments, norm_gains, gain_moments,
        step_count,
    )
    rows, kv = own.shape
    block = rows // 2
    tile = pl.BlockSpec((block, kv), lambda i: (i, 0))
    row = pl.BlockSpec((1, rows), lambda i: (0, 0))
    last = pl.BlockSpec((EXTRA, kv), lambda i: (rows // EXTRA, 0))
    out_w, out_mom, out_gain, out_gain_mom = pl.pallas_call(
        final_kernel,
        grid=(rows // block,),
        in_specs=[pl.BlockSpec(memory_space=pltpu.SMEM)] + [tile] * 5 + [row] + [last] * 4,
        out_specs=[tile, tile, row, row],
        out_shape=[
            jax.ShapeDtypeStruct((rows, kv), f32),
            jax.ShapeDtypeStruct((rows, kv), bf16),
            jax.ShapeDtypeStruct((1, rows), bf16),
            jax.ShapeDtypeStruct((1, rows), bf16),
        ],
        name="final",
    )(
        took, own, mom, peer_early, swapped, peer_mom,
        norm_gains, peer_early, swapped, mom, peer_mom,
    )
    return (out_w[None], out_mom[None], out_gain, out_gain_mom)


def solution(mesh):
    in_specs = (
        P("rep", "fsdp", None),
        P("rep", "fsdp", None),
        P("rep", "fsdp", None),
        P("rep", "fsdp", None),
        P("rep", "fsdp"),
        P("rep", "fsdp"),
        P(),
    )
    out_specs = (P("rep", "fsdp", None), P("rep", "fsdp", None), P("rep", "fsdp"), P("rep", "fsdp"))
    return jax.shard_map(shards, mesh=mesh, in_specs=in_specs, out_specs=out_specs, check_vma=False)
```

```python
from functools import partial

import jax
import jax.numpy as jnp
from jax import lax
from jax.experimental import pallas as pl
from jax.experimental.pallas import tpu as pltpu
from jax.sharding import PartitionSpec as P

D = 4096

norm_eps = 1e-05
momentum_beta = 0.9
learn_weight = 0.25
learn_gain = 0.01
grad_scale = D ** (-0.5)

EXTRA = 8
ROWS = 96
f32, bf16 = jnp.float32, jnp.bfloat16


def from_peer(value, steps):
    count = lax.axis_size("rep")
    return lax.ppermute(value, "rep", [(source, (source - steps) % count) for source in range(count)])


def within_halves(value, steps):
    half = lax.axis_size("rep") // 2
    pairs = [(h * half + i, h * half + (i - steps) % half) for h in range(2) for i in range(half)]
    return lax.ppermute(value, "rep", pairs)


def swap_halves(value, low, high):
    half = lax.axis_size("rep") // 2
    pairs = [(h * half + i, (1 - h) * half + i) for h in range(2) for i in range(low, high)]
    place = lax.rem(lax.axis_index("rep"), half)
    took = (place >= low) & (place < high)
    return lax.ppermute(value, "rep", pairs), took.astype(jnp.int32).reshape(1)


def early_kernel(master_ref, gain_ref, out_ref):
    rows = master_ref.shape[0]
    out_ref[:rows, :] = master_ref[...].astype(bf16)
    out_ref[rows:, :] = jnp.broadcast_to(gain_ref[...], (EXTRA, out_ref.shape[1]))


def pack_kernel(hidden_ref, cotangent_ref, out_ref):
    parts = out_ref.shape[0]
    share = hidden_ref.shape[1] // parts
    hidden = hidden_ref[...].astype(f32)
    inv_rms = lax.rsqrt(jnp.mean(hidden * hidden, axis=-1, keepdims=True) + norm_eps)
    cotangent = cotangent_ref[...]
    for part in range(parts):
        block = hidden_ref[:, part * share : (part + 1) * share].astype(f32)
        out_ref[part, :, :share] = (block * inv_rms).astype(bf16)
        out_ref[part, :, share:] = cotangent


def grad_kernel(got_ref, master_ref, moment_ref, gain_ref, gain_moment_ref, out_ref):
    rows = master_ref.shape[0]
    total = grad_scale * lax.dot_general(
        got_ref[:, :rows],
        got_ref[:, rows:],
        (((0,), (0,)), ((), ())),
        preferred_element_type=f32,
    )
    gain = jnp.transpose(jnp.broadcast_to(gain_ref[...].astype(f32), (128, rows)))[:, :1]
    mom = momentum_beta * moment_ref[...].astype(f32) + gain * total
    out_ref[:rows, :] = mom.astype(bf16)
    add_gain = jnp.sum(master_ref[...].astype(bf16).astype(f32) * total, axis=1, keepdims=True)
    add_gain = jnp.transpose(jnp.broadcast_to(add_gain, (rows, 128)))[:1, :]
    mom_g = momentum_beta * gain_moment_ref[...].astype(f32) + add_gain
    out_ref[rows:, :] = jnp.broadcast_to(mom_g, (EXTRA, rows)).astype(bf16)


def own_step_kernel(master_ref, mom_ref, out_ref):
    rows = master_ref.shape[0]
    out_ref[...] = 0.5 * (master_ref[...] - learn_weight * mom_ref[:rows, :].astype(f32))


def final_kernel(
    took_ref, own_ref, mom_ref, kept_ref, swapped_ref, peer_mom_ref,
    gain_ref, kept_gain_ref, swapped_gain_ref, mom_g_ref, peer_mom_g_ref,
    out_w_ref, out_mom_ref, out_gain_ref, out_gain_mom_ref,
):
    peer_mom = peer_mom_ref[...].astype(f32)
    out_mom_ref[...] = (0.5 * (mom_ref[...].astype(f32) + peer_mom)).astype(bf16)

    def finish(early_ref, early_gain_ref):
        peer_step = early_ref[...].astype(f32) - learn_weight * peer_mom
        out_w_ref[...] = own_ref[...] + 0.5 * peer_step

        @pl.when(pl.program_id(0) == 0)
        def _():
            mom_g = mom_g_ref[...].astype(f32)[:1, :]
            peer_mom_g = peer_mom_g_ref[...].astype(f32)[:1, :]
            peer_gain = early_gain_ref[...].astype(f32)[:1, :]
            own = (gain_ref[...].astype(f32) - learn_gain * mom_g).astype(bf16).astype(f32)
            peer = (peer_gain - learn_gain * peer_mom_g).astype(bf16).astype(f32)
            out_gain_ref[...] = (0.5 * (own + peer)).astype(bf16)
            out_gain_mom_ref[...] = (0.5 * (mom_g + peer_mom_g)).astype(bf16)

    pl.when(took_ref[0] == 0)(partial(finish, kept_ref, kept_gain_ref))
    pl.when(took_ref[0] != 0)(partial(finish, swapped_ref, swapped_gain_ref))


VMEM = pl.BlockSpec(memory_space=pltpu.VMEM)


def whole(distance, hidden_in, cotangent, weights, moments, norm_gains, gain_moments, step_count):
    inputs, upstream, master, moment = hidden_in[0], cotangent[0], weights[0], moments[0]
    tokens, width = inputs.shape
    rows, kv = master.shape
    parts = lax.axis_size("fsdp")
    far = distance * 2 == lax.axis_size("rep")
    far_along = 8 <= distance and not far
    early = pl.pallas_call(
        early_kernel,
        out_shape=jax.ShapeDtypeStruct((rows + EXTRA, kv), bf16),
        name="early",
    )(master, norm_gains)
    half = lax.axis_size("rep") // 2
    if far:
        peer_early = from_peer(early, distance)
    elif distance == 1:
        swapped, took = swap_halves(early, 0, distance)
        peer_early = within_halves(jnp.where(took != 0, swapped, early), distance)
        swapped, took = early, jnp.zeros_like(took)
    else:
        peer_early = within_halves(early, distance)

    def own_step(master, mom):
        return pl.pallas_call(
            own_step_kernel,
            out_shape=jax.ShapeDtypeStruct((rows, kv), f32),
            name="own",
        )(master, mom)

    def between(first, master, mom, peer_early):
        if first:
            peer_early, master = lax.optimization_barrier((peer_early, master))
        swapped, took = swap_halves(peer_early, half - distance, half)
        return own_step(master, mom), swapped, took

    def section(block, *operands):
        inputs, upstream, master, moment, norm_gains, gain_moments = operands[:6]
        packed = pl.pallas_call(
            pack_kernel,
            grid=(tokens // block,),
            in_specs=[
                pl.BlockSpec((block, width), lambda i: (i, 0)),
                pl.BlockSpec((block, kv), lambda i: (i, 0)),
            ],
            out_specs=pl.BlockSpec((parts, block, rows + kv), lambda i: (0, i, 0)),
            out_shape=jax.ShapeDtypeStruct((parts, tokens, rows + kv), bf16),
            name="pack",
        )(inputs, upstream)
        got = lax.all_to_all(packed, "fsdp", split_axis=0, concat_axis=0, tiled=True)
        got = got.reshape(parts * tokens, rows + kv)
        early = operands[6:]
        if early:
            got, *early = lax.optimization_barrier((got, *early))
        got = pltpu.with_memory_space_constraint(got, pltpu.VMEM)
        mom = pl.pallas_call(
            grad_kernel,
            in_specs=[VMEM] * 5,
            out_specs=VMEM,
            out_shape=jax.ShapeDtypeStruct((rows + EXTRA, kv), bf16),
            name="grad",
        )(got, master, moment, norm_gains, gain_moments)
        return (mom, *early)

    operands = (inputs, upstream, master, moment, norm_gains, gain_moments)
    if far_along:
        (mom,) = section(ROWS, *operands)
        peer_mom = from_peer(mom, distance)
        sure = step_count >= 0
        own, swapped, took = lax.cond(
            sure, partial(between, True), partial(between, False), master, mom, peer_early
        )
        peer_mom, own = lax.optimization_barrier((peer_mom, own))
    elif far:
        (mom,) = section(ROWS, *operands)
        swapped, took = early, jnp.zeros((1,), jnp.int32)
    elif distance == 1:
        (mom,) = section(ROWS, *operands)
    else:
        mom, peer_early = section(ROWS, *operands, peer_early)
        swapped, took = swap_halves(peer_early, half - distance, half)
        if distance == 2:
            peer_early, took = jnp.where(took != 0, swapped, peer_early), jnp.zeros_like(took)
    if not far_along:
        peer_mom = from_peer(mom, distance)
        own = own_step(master, mom)
    return own, mom, peer_mom, peer_early, swapped, took


def shards(hidden_in, cotangent, weights, moments, norm_gains, gain_moments, step_count):
    hop_total = lax.axis_size("rep").bit_length() - 1
    hop_index = lax.rem(step_count, hop_total)
    branches = [partial(whole, 1 << level) for level in range(hop_total)]
    own, mom, peer_mom, peer_early, swapped, took = lax.switch(
        hop_index, branches, hidden_in, cotangent, weights, moments, norm_gains, gain_moments,
        step_count,
    )
    rows, kv = own.shape
    block = rows // 2
    tile = pl.BlockSpec((block, kv), lambda i: (i, 0))
    row = pl.BlockSpec((1, rows), lambda i: (0, 0))
    last = pl.BlockSpec((EXTRA, kv), lambda i: (rows // EXTRA, 0))
    out_w, out_mom, out_gain, out_gain_mom = pl.pallas_call(
        final_kernel,
        grid=(rows // block,),
        in_specs=[pl.BlockSpec(memory_space=pltpu.SMEM)] + [tile] * 5 + [row] + [last] * 4,
        out_specs=[tile, tile, row, row],
        out_shape=[
            jax.ShapeDtypeStruct((rows, kv), f32),
            jax.ShapeDtypeStruct((rows, kv), bf16),
            jax.ShapeDtypeStruct((1, rows), bf16),
            jax.ShapeDtypeStruct((1, rows), bf16),
        ],
        name="final",
    )(
        took, own, mom, peer_early, swapped, peer_mom,
        norm_gains, peer_early, swapped, mom, peer_mom,
    )
    return (out_w[None], out_mom[None], out_gain, out_gain_mom)


def solution(mesh):
    in_specs = (
        P("rep", "fsdp", None),
        P("rep", "fsdp", None),
        P("rep", "fsdp", None),
        P("rep", "fsdp", None),
        P("rep", "fsdp"),
        P("rep", "fsdp"),
        P(),
    )
    out_specs = (P("rep", "fsdp", None), P("rep", "fsdp", None), P("rep", "fsdp"), P("rep", "fsdp"))
    return jax.shard_map(shards, mesh=mesh, in_specs=in_specs, out_specs=out_specs, check_vma=False)
```

```python
from functools import partial

import jax
import jax.numpy as jnp
from jax import lax
from jax.experimental import pallas as pl
from jax.experimental.pallas import tpu as pltpu
from jax.sharding import PartitionSpec as P

D = 4096

norm_eps = 1e-05
momentum_beta = 0.9
learn_weight = 0.25
learn_gain = 0.01
grad_scale = D ** (-0.5)

EXTRA = 8
ROWS = 96
f32, bf16 = jnp.float32, jnp.bfloat16


def from_peer(value, steps):
    count = lax.axis_size("rep")
    return lax.ppermute(value, "rep", [(source, (source - steps) % count) for source in range(count)])


def within_halves(value, steps):
    half = lax.axis_size("rep") // 2
    pairs = [(h * half + i, h * half + (i - steps) % half) for h in range(2) for i in range(half)]
    return lax.ppermute(value, "rep", pairs)


def swap_halves(value, low, high):
    half = lax.axis_size("rep") // 2
    pairs = [(h * half + i, (1 - h) * half + i) for h in range(2) for i in range(low, high)]
    place = lax.rem(lax.axis_index("rep"), half)
    took = (place >= low) & (place < high)
    return lax.ppermute(value, "rep", pairs), took.astype(jnp.int32).reshape(1)


def early_kernel(master_ref, gain_ref, out_ref):
    rows = master_ref.shape[0]
    out_ref[:rows, :] = master_ref[...].astype(bf16)
    out_ref[rows:, :] = jnp.broadcast_to(gain_ref[...], (EXTRA, out_ref.shape[1]))


def pack_kernel(hidden_ref, cotangent_ref, out_ref):
    parts = out_ref.shape[0]
    share = hidden_ref.shape[1] // parts
    hidden = hidden_ref[...].astype(f32)
    inv_rms = lax.rsqrt(jnp.mean(hidden * hidden, axis=-1, keepdims=True) + norm_eps)
    cotangent = cotangent_ref[...]
    for part in range(parts):
        block = hidden_ref[:, part * share : (part + 1) * share].astype(f32)
        out_ref[part, :, :share] = (block * inv_rms).astype(bf16)
        out_ref[part, :, share:] = cotangent


def grad_kernel(got_ref, master_ref, moment_ref, gain_ref, gain_moment_ref, out_ref):
    rows = master_ref.shape[0]
    total = grad_scale * lax.dot_general(
        got_ref[:, :rows],
        got_ref[:, rows:],
        (((0,), (0,)), ((), ())),
        preferred_element_type=f32,
    )
    gain = jnp.transpose(jnp.broadcast_to(gain_ref[...].astype(f32), (128, rows)))[:, :1]
    mom = momentum_beta * moment_ref[...].astype(f32) + gain * total
    out_ref[:rows, :] = mom.astype(bf16)
    add_gain = jnp.sum(master_ref[...].astype(bf16).astype(f32) * total, axis=1, keepdims=True)
    add_gain = jnp.transpose(jnp.broadcast_to(add_gain, (rows, 128)))[:1, :]
    mom_g = momentum_beta * gain_moment_ref[...].astype(f32) + add_gain
    out_ref[rows:, :] = jnp.broadcast_to(mom_g, (EXTRA, rows)).astype(bf16)


def own_step_kernel(master_ref, mom_ref, out_ref):
    rows = master_ref.shape[0]
    out_ref[...] = 0.5 * (master_ref[...] - learn_weight * mom_ref[:rows, :].astype(f32))


def final_kernel(
    took_ref, own_ref, mom_ref, kept_ref, swapped_ref, peer_mom_ref,
    gain_ref, kept_gain_ref, swapped_gain_ref, mom_g_ref, peer_mom_g_ref,
    out_w_ref, out_mom_ref, out_gain_ref, out_gain_mom_ref,
):
    peer_mom = peer_mom_ref[...].astype(f32)
    out_mom_ref[...] = (0.5 * (mom_ref[...].astype(f32) + peer_mom)).astype(bf16)

    def finish(early_ref, early_gain_ref):
        peer_step = early_ref[...].astype(f32) - learn_weight * peer_mom
        out_w_ref[...] = own_ref[...] + 0.5 * peer_step

        @pl.when(pl.program_id(0) == 0)
        def _():
            mom_g = mom_g_ref[...].astype(f32)[:1, :]
            peer_mom_g = peer_mom_g_ref[...].astype(f32)[:1, :]
            peer_gain = early_gain_ref[...].astype(f32)[:1, :]
            own = (gain_ref[...].astype(f32) - learn_gain * mom_g).astype(bf16).astype(f32)
            peer = (peer_gain - learn_gain * peer_mom_g).astype(bf16).astype(f32)
            out_gain_ref[...] = (0.5 * (own + peer)).astype(bf16)
            out_gain_mom_ref[...] = (0.5 * (mom_g + peer_mom_g)).astype(bf16)

    pl.when(took_ref[0] == 0)(partial(finish, kept_ref, kept_gain_ref))
    pl.when(took_ref[0] != 0)(partial(finish, swapped_ref, swapped_gain_ref))


VMEM = pl.BlockSpec(memory_space=pltpu.VMEM)


def whole(distance, hidden_in, cotangent, weights, moments, norm_gains, gain_moments, step_count):
    inputs, upstream, master, moment = hidden_in[0], cotangent[0], weights[0], moments[0]
    tokens, width = inputs.shape
    rows, kv = master.shape
    parts = lax.axis_size("fsdp")
    far = distance * 2 == lax.axis_size("rep")
    swaps_inside = (8 <= distance or distance == 2) and not far
    early = pl.pallas_call(
        early_kernel,
        out_shape=jax.ShapeDtypeStruct((rows + EXTRA, kv), bf16),
        name="early",
    )(master, norm_gains)
    half = lax.axis_size("rep") // 2
    if far:
        peer_early = from_peer(early, distance)
    elif distance <= 2:
        swapped, took = swap_halves(early, 0, 1)
        peer_early = within_halves(jnp.where(took != 0, swapped, early), distance)
        swapped, took = early, jnp.zeros_like(took)
    else:
        peer_early = within_halves(early, distance)

    def own_step(master, mom):
        return pl.pallas_call(
            own_step_kernel,
            out_shape=jax.ShapeDtypeStruct((rows, kv), f32),
            name="own",
        )(master, mom)

    def between(first, master, mom, peer_early):
        if first:
            peer_early, master = lax.optimization_barrier((peer_early, master))
        low = half - distance if distance > 2 else half - distance + 1
        swapped, took = swap_halves(peer_early, low, half)
        return own_step(master, mom), swapped, took

    def section(block, *operands):
        inputs, upstream, master, moment, norm_gains, gain_moments = operands[:6]
        packed = pl.pallas_call(
            pack_kernel,
            grid=(tokens // block,),
            in_specs=[
                pl.BlockSpec((block, width), lambda i: (i, 0)),
                pl.BlockSpec((block, kv), lambda i: (i, 0)),
            ],
            out_specs=pl.BlockSpec((parts, block, rows + kv), lambda i: (0, i, 0)),
            out_shape=jax.ShapeDtypeStruct((parts, tokens, rows + kv), bf16),
            name="pack",
        )(inputs, upstream)
        got = lax.all_to_all(packed, "fsdp", split_axis=0, concat_axis=0, tiled=True)
        got = got.reshape(parts * tokens, rows + kv)
        early = operands[6:]
        if early:
            got, *early = lax.optimization_barrier((got, *early))
        got = pltpu.with_memory_space_constraint(got, pltpu.VMEM)
        mom = pl.pallas_call(
            grad_kernel,
            in_specs=[VMEM] * 5,
            out_specs=VMEM,
            out_shape=jax.ShapeDtypeStruct((rows + EXTRA, kv), bf16),
            name="grad",
        )(got, master, moment, norm_gains, gain_moments)
        return (mom, *early)

    operands = (inputs, upstream, master, moment, norm_gains, gain_moments)
    if swaps_inside:
        (mom,) = section(ROWS, *operands)
        peer_mom = from_peer(mom, distance)
        sure = step_count >= 0
        own, swapped, took = lax.cond(
            sure, partial(between, True), partial(between, False), master, mom, peer_early
        )
        peer_mom, own = lax.optimization_barrier((peer_mom, own))
    elif far:
        (mom,) = section(ROWS, *operands)
        swapped, took = early, jnp.zeros((1,), jnp.int32)
    elif distance == 1:
        (mom,) = section(ROWS, *operands)
    else:
        mom, peer_early = section(ROWS, *operands, peer_early)
        swapped, took = swap_halves(peer_early, half - distance, half)
    if not swaps_inside:
        peer_mom = from_peer(mom, distance)
        own = own_step(master, mom)
    return own, mom, peer_mom, peer_early, swapped, took


def shards(hidden_in, cotangent, weights, moments, norm_gains, gain_moments, step_count):
    hop_total = lax.axis_size("rep").bit_length() - 1
    hop_index = lax.rem(step_count, hop_total)
    branches = [partial(whole, 1 << level) for level in range(hop_total)]
    own, mom, peer_mom, peer_early, swapped, took = lax.switch(
        hop_index, branches, hidden_in, cotangent, weights, moments, norm_gains, gain_moments,
        step_count,
    )
    rows, kv = own.shape
    block = rows // 2
    tile = pl.BlockSpec((block, kv), lambda i: (i, 0))
    row = pl.BlockSpec((1, rows), lambda i: (0, 0))
    last = pl.BlockSpec((EXTRA, kv), lambda i: (rows // EXTRA, 0))
    out_w, out_mom, out_gain, out_gain_mom = pl.pallas_call(
        final_kernel,
        grid=(rows // block,),
        in_specs=[pl.BlockSpec(memory_space=pltpu.SMEM)] + [tile] * 5 + [row] + [last] * 4,
        out_specs=[tile, tile, row, row],
        out_shape=[
            jax.ShapeDtypeStruct((rows, kv), f32),
            jax.ShapeDtypeStruct((rows, kv), bf16),
            jax.ShapeDtypeStruct((1, rows), bf16),
            jax.ShapeDtypeStruct((1, rows), bf16),
        ],
        name="final",
    )(
        took, own, mom, peer_early, swapped, peer_mom,
        norm_gains, peer_early, swapped, mom, peer_mom,
    )
    return (out_w[None], out_mom[None], out_gain, out_gain_mom)


def solution(mesh):
    in_specs = (
        P("rep", "fsdp", None),
        P("rep", "fsdp", None),
        P("rep", "fsdp", None),
        P("rep", "fsdp", None),
        P("rep", "fsdp"),
        P("rep", "fsdp"),
        P(),
    )
    out_specs = (P("rep", "fsdp", None), P("rep", "fsdp", None), P("rep", "fsdp"), P("rep", "fsdp"))
    return jax.shard_map(shards, mesh=mesh, in_specs=in_specs, out_specs=out_specs, check_vma=False)
```

```python
from functools import partial

import jax
import jax.numpy as jnp
from jax import lax
from jax.experimental import pallas as pl
from jax.experimental.pallas import tpu as pltpu
from jax.sharding import PartitionSpec as P

D = 4096

norm_eps = 1e-05
momentum_beta = 0.9
learn_weight = 0.25
learn_gain = 0.01
grad_scale = D ** (-0.5)

EXTRA = 8
ROWS = 96
f32, bf16 = jnp.float32, jnp.bfloat16


def from_peer(value, steps):
    count = lax.axis_size("rep")
    return lax.ppermute(value, "rep", [(source, (source - steps) % count) for source in range(count)])


def within_halves(value, steps):
    half = lax.axis_size("rep") // 2
    pairs = [(h * half + i, h * half + (i - steps) % half) for h in range(2) for i in range(half)]
    return lax.ppermute(value, "rep", pairs)


def swap_halves(value, low, high):
    half = lax.axis_size("rep") // 2
    pairs = [(h * half + i, (1 - h) * half + i) for h in range(2) for i in range(low, high)]
    place = lax.rem(lax.axis_index("rep"), half)
    took = (place >= low) & (place < high)
    return lax.ppermute(value, "rep", pairs), took.astype(jnp.int32).reshape(1)


def early_kernel(master_ref, gain_ref, out_ref):
    rows = master_ref.shape[0]
    out_ref[:rows, :] = master_ref[...].astype(bf16)
    out_ref[rows:, :] = jnp.broadcast_to(gain_ref[...], (EXTRA, out_ref.shape[1]))


def pack_kernel(hidden_ref, cotangent_ref, out_ref):
    parts = out_ref.shape[0]
    share = hidden_ref.shape[1] // parts
    hidden = hidden_ref[...].astype(f32)
    inv_rms = lax.rsqrt(jnp.mean(hidden * hidden, axis=-1, keepdims=True) + norm_eps)
    cotangent = cotangent_ref[...]
    for part in range(parts):
        block = hidden_ref[:, part * share : (part + 1) * share].astype(f32)
        out_ref[part, :, :share] = (block * inv_rms).astype(bf16)
        out_ref[part, :, share:] = cotangent


def grad_kernel(got_ref, master_ref, moment_ref, gain_ref, gain_moment_ref, out_ref):
    rows = master_ref.shape[0]
    total = grad_scale * lax.dot_general(
        got_ref[:, :rows],
        got_ref[:, rows:],
        (((0,), (0,)), ((), ())),
        preferred_element_type=f32,
    )
    gain = jnp.transpose(jnp.broadcast_to(gain_ref[...].astype(f32), (128, rows)))[:, :1]
    mom = momentum_beta * moment_ref[...].astype(f32) + gain * total
    out_ref[:rows, :] = mom.astype(bf16)
    add_gain = jnp.sum(master_ref[...].astype(bf16).astype(f32) * total, axis=1, keepdims=True)
    add_gain = jnp.transpose(jnp.broadcast_to(add_gain, (rows, 128)))[:1, :]
    mom_g = momentum_beta * gain_moment_ref[...].astype(f32) + add_gain
    out_ref[rows:, :] = jnp.broadcast_to(mom_g, (EXTRA, rows)).astype(bf16)


def own_step_kernel(master_ref, mom_ref, out_ref):
    rows = master_ref.shape[0]
    out_ref[...] = 0.5 * (master_ref[...] - learn_weight * mom_ref[:rows, :].astype(f32))


def final_kernel(
    took_ref, own_ref, mom_ref, kept_ref, swapped_ref, peer_mom_ref,
    gain_ref, kept_gain_ref, swapped_gain_ref, mom_g_ref, peer_mom_g_ref,
    out_w_ref, out_mom_ref, out_gain_ref, out_gain_mom_ref,
):
    peer_mom = peer_mom_ref[...].astype(f32)
    out_mom_ref[...] = (0.5 * (mom_ref[...].astype(f32) + peer_mom)).astype(bf16)

    def finish(early_ref, early_gain_ref):
        peer_step = early_ref[...].astype(f32) - learn_weight * peer_mom
        out_w_ref[...] = own_ref[...] + 0.5 * peer_step

        @pl.when(pl.program_id(0) == 0)
        def _():
            mom_g = mom_g_ref[...].astype(f32)[:1, :]
            peer_mom_g = peer_mom_g_ref[...].astype(f32)[:1, :]
            peer_gain = early_gain_ref[...].astype(f32)[:1, :]
            own = (gain_ref[...].astype(f32) - learn_gain * mom_g).astype(bf16).astype(f32)
            peer = (peer_gain - learn_gain * peer_mom_g).astype(bf16).astype(f32)
            out_gain_ref[...] = (0.5 * (own + peer)).astype(bf16)
            out_gain_mom_ref[...] = (0.5 * (mom_g + peer_mom_g)).astype(bf16)

    pl.when(took_ref[0] == 0)(partial(finish, kept_ref, kept_gain_ref))
    pl.when(took_ref[0] != 0)(partial(finish, swapped_ref, swapped_gain_ref))


VMEM = pl.BlockSpec(memory_space=pltpu.VMEM)


def whole(distance, hidden_in, cotangent, weights, moments, norm_gains, gain_moments, step_count):
    inputs, upstream, master, moment = hidden_in[0], cotangent[0], weights[0], moments[0]
    tokens, width = inputs.shape
    rows, kv = master.shape
    parts = lax.axis_size("fsdp")
    far = distance * 2 == lax.axis_size("rep")
    swaps_inside = 2 <= distance and not far
    early = pl.pallas_call(
        early_kernel,
        out_shape=jax.ShapeDtypeStruct((rows + EXTRA, kv), bf16),
        name="early",
    )(master, norm_gains)
    half = lax.axis_size("rep") // 2
    if far:
        peer_early = from_peer(early, distance)
    elif distance <= 2:
        swapped, took = swap_halves(early, 0, 1)
        peer_early = within_halves(jnp.where(took != 0, swapped, early), distance)
        swapped, took = early, jnp.zeros_like(took)
    else:
        peer_early = within_halves(early, distance)

    def own_step(master, mom):
        return pl.pallas_call(
            own_step_kernel,
            out_shape=jax.ShapeDtypeStruct((rows, kv), f32),
            name="own",
        )(master, mom)

    def between(first, master, mom, peer_early):
        if first:
            peer_early, master = lax.optimization_barrier((peer_early, master))
        low = half - distance if distance > 2 else half - distance + 1
        swapped, took = swap_halves(peer_early, low, half)
        return own_step(master, mom), swapped, took

    def section(block, *operands):
        inputs, upstream, master, moment, norm_gains, gain_moments = operands[:6]
        packed = pl.pallas_call(
            pack_kernel,
            grid=(tokens // block,),
            in_specs=[
                pl.BlockSpec((block, width), lambda i: (i, 0)),
                pl.BlockSpec((block, kv), lambda i: (i, 0)),
            ],
            out_specs=pl.BlockSpec((parts, block, rows + kv), lambda i: (0, i, 0)),
            out_shape=jax.ShapeDtypeStruct((parts, tokens, rows + kv), bf16),
            name="pack",
        )(inputs, upstream)
        got = lax.all_to_all(packed, "fsdp", split_axis=0, concat_axis=0, tiled=True)
        got = got.reshape(parts * tokens, rows + kv)
        early = operands[6:]
        if early:
            got, *early = lax.optimization_barrier((got, *early))
        got = pltpu.with_memory_space_constraint(got, pltpu.VMEM)
        mom = pl.pallas_call(
            grad_kernel,
            in_specs=[VMEM] * 5,
            out_specs=VMEM,
            out_shape=jax.ShapeDtypeStruct((rows + EXTRA, kv), bf16),
            name="grad",
        )(got, master, moment, norm_gains, gain_moments)
        return (mom, *early)

    operands = (inputs, upstream, master, moment, norm_gains, gain_moments)
    if swaps_inside:
        (mom,) = section(ROWS, *operands)
        peer_mom = from_peer(mom, distance)
        sure = step_count >= 0
        own, swapped, took = lax.cond(
            sure, partial(between, True), partial(between, False), master, mom, peer_early
        )
        peer_mom, own = lax.optimization_barrier((peer_mom, own))
    elif far:
        (mom,) = section(ROWS, *operands)
        swapped, took = early, jnp.zeros((1,), jnp.int32)
    elif distance == 1:
        (mom,) = section(ROWS, *operands)
    else:
        mom, peer_early = section(ROWS, *operands, peer_early)
        swapped, took = swap_halves(peer_early, half - distance, half)
    if not swaps_inside:
        peer_mom = from_peer(mom, distance)
        own = own_step(master, mom)
    return own, mom, peer_mom, peer_early, swapped, took


def shards(hidden_in, cotangent, weights, moments, norm_gains, gain_moments, step_count):
    hop_total = lax.axis_size("rep").bit_length() - 1
    hop_index = lax.rem(step_count, hop_total)
    branches = [partial(whole, 1 << level) for level in range(hop_total)]
    own, mom, peer_mom, peer_early, swapped, took = lax.switch(
        hop_index, branches, hidden_in, cotangent, weights, moments, norm_gains, gain_moments,
        step_count,
    )
    rows, kv = own.shape
    block = rows // 2
    tile = pl.BlockSpec((block, kv), lambda i: (i, 0))
    row = pl.BlockSpec((1, rows), lambda i: (0, 0))
    last = pl.BlockSpec((EXTRA, kv), lambda i: (rows // EXTRA, 0))
    out_w, out_mom, out_gain, out_gain_mom = pl.pallas_call(
        final_kernel,
        grid=(rows // block,),
        in_specs=[pl.BlockSpec(memory_space=pltpu.SMEM)] + [tile] * 5 + [row] + [last] * 4,
        out_specs=[tile, tile, row, row],
        out_shape=[
            jax.ShapeDtypeStruct((rows, kv), f32),
            jax.ShapeDtypeStruct((rows, kv), bf16),
            jax.ShapeDtypeStruct((1, rows), bf16),
            jax.ShapeDtypeStruct((1, rows), bf16),
        ],
        name="final",
    )(
        took, own, mom, peer_early, swapped, peer_mom,
        norm_gains, peer_early, swapped, mom, peer_mom,
    )
    return (out_w[None], out_mom[None], out_gain, out_gain_mom)


def solution(mesh):
    in_specs = (
        P("rep", "fsdp", None),
        P("rep", "fsdp", None),
        P("rep", "fsdp", None),
        P("rep", "fsdp", None),
        P("rep", "fsdp"),
        P("rep", "fsdp"),
        P(),
    )
    out_specs = (P("rep", "fsdp", None), P("rep", "fsdp", None), P("rep", "fsdp"), P("rep", "fsdp"))
    return jax.shard_map(shards, mesh=mesh, in_specs=in_specs, out_specs=out_specs, check_vma=False)
```
